32 devices in a mesh: grp: 8 (over z, x), blk: 4 (over y, core).
Axes of the slice: x: 2, y: 2, z: 4, core: 2. Of those that a mesh axis runs over, the one named last changes fastest.
Arguments:
- embeddings: bfloat16 [16384, 1024], P(('grp', 'blk')), may hold values from -60 to 60
- cluster_ids: int32 [16384], P(('grp', 'blk')), may hold values from 0 to 7, as said below
- rank_key: int32 [16384], P(('grp', 'blk')), may hold values from 0 to 16383, each once
Outputs:
- best: float32 [16384], P(('grp', 'blk'))
The draws below stay inside these ranges and needn't reach their ends.
Inputs may be any that keep to these rules, and one draw needn't show every extreme that they name: `cluster_ids`: on every device, at most 128 of its rows have cluster ids congruent to one value modulo 8, and for some value exactly that many.
All inputs are finite; a program needn't handle non-finite values.
Results may differ from the reference program's by a relative error of at most 0.0005.
Values may be sent and summed in bfloat16 or wider, within the bound.
No kernel may reach another device: no remote copies, remote signals or barrier semaphores. Data moves between devices by JAX's collectives and lax.ppermute only.
A program may use at most 64 MiB of HBM per device.

```python
import math
import jax
import jax.numpy as jnp
from jax import lax

D = 1024
ROWS_DEV = 512
CL_GRP = 1
ROWS = 16384
N_GRP = 8
N_BLK = 4


def cluster_layout(key):
    devices = N_GRP * N_BLK
    room = 2 * ROWS_DEV // N_GRP
    k_hot, k_pick, k_slot, k_within = jax.random.split(jax.random.fold_in(key, 11), 4)
    hot = jax.random.permutation(k_hot, N_GRP)[:2]
    full_group = hot[jax.random.randint(k_pick, (devices,), 0, 2)]

    def device_rows(dkey, favoured):
        k_first, k_second = jax.random.split(dkey)
        shuffled = jax.random.permutation(k_first, 2 * ROWS_DEV).astype(jnp.int32)
        owner_of = shuffled // room
        score = jnp.where(owner_of == favoured, 0, 1) * (2 * ROWS_DEV) + jnp.arange(2 * ROWS_DEV, dtype=jnp.int32)
        picked = shuffled[jnp.argsort(score)[:ROWS_DEV]]
        mixed = jax.random.permutation(k_second, picked)
        return mixed // room
    owners = jax.vmap(device_rows)(jax.random.split(k_slot, devices), full_group).reshape(-1)
    within = jnp.min(jax.random.randint(k_within, (3, ROWS_DEV * devices), 0, CL_GRP), axis=0)
    return (owners + N_GRP * within).astype(jnp.int32)


def pair_layout(key, clusters):
    total = clusters.shape[0]
    k_order, k_flag = jax.random.split(jax.random.fold_in(key, 37))
    shuffled = jax.random.permutation(k_order, total).astype(jnp.int32)
    sort_key = clusters * total + shuffled
    order = jnp.argsort(sort_key).astype(jnp.int32)
    position = jnp.zeros((total,), jnp.int32).at[order].set(jnp.arange(total, dtype=jnp.int32))
    mate = order[jnp.bitwise_xor(position, 1)]
    leader = order[position // 2 * 2]
    flags = jax.random.randint(k_flag, (total // 2,), 0, 2)
    paired = (clusters[mate] == clusters) & (flags[position // 2] == 1)
    return (paired, leader)


def draw_cluster_ids(key, part):
    return cluster_layout(key)


def draw_embeddings(key, part):
    clusters = cluster_layout(key)
    total = clusters.shape[0]
    paired, leader = pair_layout(key, clusters)
    k_centre = jax.random.fold_in(jax.random.fold_in(key, 23), 0)
    k_weight = jax.random.fold_in(jax.random.fold_in(key, 23), 1)
    k_noise = jax.random.fold_in(jax.random.fold_in(key, 23), 2)
    k_extra = jax.random.fold_in(jax.random.fold_in(key, 23), 4)
    centres = jax.random.normal(k_centre, (CL_GRP * N_GRP, D), jnp.float32)
    weight = jax.random.uniform(k_weight, (total, 1), jnp.float32, 0.1, 1.0)
    noise = jax.random.normal(k_noise, (total, D), jnp.float32)
    extra = jax.random.normal(k_extra, (total, D), jnp.float32)
    shared = jnp.where(paired[:, None], noise[leader] + 0.2 * extra, noise)
    values = weight * centres[clusters] + shared
    return jnp.clip(values, -60.0, 60.0).astype(jnp.bfloat16)


def setup_inputs(seed: int = 0) -> dict:
    key_list = jax.random.split(jax.random.key(seed), 4)
    embeddings = draw_embeddings(jax.random.fold_in(key_list[3], 71), 0)
    cluster_ids = draw_cluster_ids(jax.random.fold_in(key_list[3], 71), 0)
    rank_key = jax.random.permutation(key_list[2], ROWS).astype(jnp.int32)
    return dict(embeddings=embeddings, cluster_ids=cluster_ids, rank_key=rank_key)


epsilon = 1e-06

def reference(embeddings, cluster_ids, rank_key):
    total = embeddings.shape[0]
    values = embeddings.astype(jnp.float32)
    squares = lax.optimization_barrier(jnp.sum(values * values, axis=1, keepdims=True))
    unit = (values * lax.rsqrt(squares + epsilon)).astype(jnp.bfloat16)
    unit = lax.optimization_barrier(unit).astype(jnp.float32)
    room = 2 * ROWS_DEV * N_BLK
    width = math.gcd(room, 512)
    count = room // width

    def one_group(owner_index):
        member = cluster_ids % N_GRP == owner_index
        pick = jnp.argsort(jnp.where(member, 0, 1).astype(jnp.int32), stable=True)[:room].astype(jnp.int32)
        valid = member[pick]
        group_unit = unit[pick]
        group_cluster = jnp.where(valid, cluster_ids[pick], -1)
        group_rank = rank_key[pick]

        def query_block(index):
            start = (index * width).astype(jnp.int32)
            query = lax.dynamic_slice_in_dim(group_unit, start, width, 0)
            query_cluster = lax.dynamic_slice_in_dim(group_cluster, start, width, 0)
            query_rank = lax.dynamic_slice_in_dim(group_rank, start, width, 0)
            score = jnp.dot(query, group_unit.T, precision=lax.Precision.HIGHEST)
            keep = (query_cluster[:, None] == group_cluster[None, :]) & (group_cluster[None, :] >= 0) & (group_rank[None, :] < query_rank[:, None])
            return lax.optimization_barrier(jnp.max(jnp.where(keep, score, -1.0), axis=1))
        found = lax.map(query_block, jnp.arange(count, dtype=jnp.int32)).reshape(room)
        return (pick, valid, found)
    picks, valids, founds = lax.map(one_group, jnp.arange(N_GRP, dtype=jnp.int32))
    places = jnp.where(valids, picks, total).reshape(-1)
    best = jnp.full((total,), -1.0, jnp.float32)
    return best.at[places].set(founds.reshape(-1), mode='drop')
```

```python
import functools
import jax
import jax.numpy as jnp
from jax import lax
from jax.experimental import pallas as pl
from jax.experimental.pallas import tpu as pltpu
from jax.sharding import PartitionSpec as P


epsilon = 1e-06
AXES = ("grp", "blk")
META = 16
LANES = 128
VMEM_LIMIT = 60 * 1024 * 1024


def physical(mesh):
    groups, members = mesh.shape["grp"], mesh.shape["blk"]
    devices = mesh.devices.reshape(groups, members)
    try:
        z = len({d.coords[2] for d in devices[:, 0]})
        core = len({d.core_on_chip for d in devices[0]})
    except (AttributeError, TypeError, IndexError):
        z, core = groups, 1
    return z, groups // z, members // core, core


def prepare_kernel(emb_ref, cluster_ref, rank_ref, whole_ref, low_ref, high_ref):
    rows = emb_ref.shape[0]
    half = rows // 2
    width = emb_ref.shape[1]
    for start in range(0, rows, LANES):
        values = emb_ref[start : start + LANES, :].astype(jnp.float32)
        squares = jnp.sum(values * values, axis=1, keepdims=True)
        unit = (values * lax.rsqrt(squares + epsilon)).astype(jnp.bfloat16)
        whole_ref[start : start + LANES, :] = unit
        if start < half:
            low_ref[start : start + LANES, :] = unit
        else:
            high_ref[start - half : start - half + LANES, :] = unit
    cluster = cluster_ref[...] + 1
    rank = rank_ref[...]
    line = lax.broadcasted_iota(jnp.int32, (META, rows), 0)
    digits = jnp.where(
        line == 0,
        cluster,
        jnp.where(line == 1, rank & 255, jnp.where(line == 2, (rank >> 8) & 255, rank >> 16)),
    )
    meta = jnp.where(line < 4, digits, 0).astype(jnp.float32).astype(jnp.bfloat16)
    whole_ref[rows : rows + META, :] = jnp.zeros((META, width), jnp.bfloat16)
    whole_ref[rows : rows + META, :rows] = meta
    high_ref[half : half + META, :] = jnp.zeros((META, width), jnp.bfloat16)
    high_ref[half : half + META, :rows] = meta


def prepare(embeddings, cluster_ids, rank_key):
    rows, width = embeddings.shape
    half = rows // 2
    return pl.pallas_call(
        prepare_kernel,
        out_shape=(
            jax.ShapeDtypeStruct((rows + META, width), jnp.bfloat16),
            jax.ShapeDtypeStruct((half, width), jnp.bfloat16),
            jax.ShapeDtypeStruct((half + META, width), jnp.bfloat16),
        ),
        name="prepare",
    )(embeddings, cluster_ids.reshape(1, rows), rank_key.reshape(1, rows))


def labels(meta):
    lines = meta.astype(jnp.float32)
    return lines[0:1], lines[1:2] + 256.0 * lines[2:3] + 65536.0 * lines[3:4]


def columns(line):
    parts = [
        jnp.transpose(jnp.broadcast_to(line[:, i : i + LANES], (LANES, LANES)))
        for i in range(0, line.shape[1], LANES)
    ]
    return jnp.concatenate(parts, axis=0)


def pairs_kernel(pieces, queries, both, tile, *refs):
    count = len(pieces)
    flat = [(b, at, n) for b, parts in enumerate(pieces) for at, n in parts]
    refs = list(refs)
    blocks = [refs.pop(0) for _ in flat]
    query_refs = [refs.pop(0) for _ in queries]
    meta_refs = [refs.pop(0) if q[2] else None for q in queries]
    any_both = any(both)
    out_blocks = refs.pop(0) if any_both else None
    out_queries = [refs.pop(0) for _ in queries]
    held, sem = refs.pop(0), refs.pop(0)
    tops = [refs.pop(0) for _ in queries]
    for (b, at, n), ref in zip(flat, blocks):
        pltpu.make_async_copy(ref, held.at[b, pl.ds(at, n), :], sem.at[b]).start()
    rows = held.shape[1] - META
    facts = []
    for (n, first, _), ref, meta, top in zip(queries, query_refs, meta_refs, tops):
        source = ref if meta is None else meta
        end = source.shape[0]
        cluster, rank = labels(source[end - META : end, first : first + n])
        facts.append((cluster, rank))
        top[...] = jnp.full(top.shape, -1.0, jnp.float32)

    def step(b, carry):
        pltpu.make_async_copy(held.at[b], held.at[b], sem.at[b]).wait()
        for start in range(0, rows, tile):
            block = held[b, start : start + tile, :]
            cluster, rank = labels(held[b, rows : rows + META, start : start + tile])
            cluster_a, rank_a = columns(cluster), columns(rank)
            best = jnp.full((tile, LANES), -1.0, jnp.float32)
            for (n, _, _), ref, (cluster_q, rank_q), two, top in zip(
                queries, query_refs, facts, both, tops
            ):
                score = lax.dot_general(
                    block,
                    ref[:n, :],
                    (((1,), (1,)), ((), ())),
                    preferred_element_type=jnp.float32,
                )
                for lane in range(0, n, LANES):
                    part = score[:, lane : lane + LANES]
                    same = cluster_a == cluster_q[:, lane : lane + LANES]
                    if two:
                        later = rank_q[:, lane : lane + LANES] < rank_a
                        part = jnp.where(same, part, -1.0)
                        best = jnp.maximum(best, jnp.where(later, part, -1.0))
                        left = jnp.where(later, -1.0, part)
                    else:
                        left = jnp.where(same & (rank_a < rank_q[:, lane : lane + LANES]), part, -1.0)
                    top[:, lane : lane + LANES] = jnp.maximum(
                        top[:, lane : lane + LANES],
                        jnp.max(left.reshape(tile // 8, 8, LANES), axis=0),
                    )
            if any_both:
                for i in range(0, tile, LANES):
                    out_blocks[b, :, start + i : start + i + LANES] = jnp.max(
                        jnp.transpose(best[i : i + LANES]), axis=0, keepdims=True
                    )
        return carry

    lax.fori_loop(0, count, step, 0)
    for top, out in zip(tops, out_queries):
        out[...] = jnp.max(top[...], axis=0, keepdims=True)


def pairs(blocks, queries, name):
    width = queries[0][0].shape[1]
    pieces, arrays = [], []
    for block in blocks:
        at, parts = 0, []
        for piece in block:
            parts.append((at, piece.shape[0]))
            arrays.append(piece)
            at += piece.shape[0]
        pieces.append(tuple(parts))
    rows = at - META
    both = tuple(q[4] for q in queries)
    metas = [q[3] for q in queries if q[3] is not None]
    kernel = functools.partial(
        pairs_kernel,
        tuple(pieces),
        tuple((q[1], q[2], q[3] is not None) for q in queries),
        both,
        min(256, rows),
    )
    outs = [jax.ShapeDtypeStruct((len(blocks), 1, rows), jnp.float32)] if any(both) else []
    outs += [jax.ShapeDtypeStruct((1, q[1]), jnp.float32) for q in queries]
    total = sum(q[1] for q in queries)
    cost = pl.CostEstimate(
        flops=2 * len(blocks) * rows * total * width,
        bytes_accessed=2 * width * (len(blocks) * rows + total),
        transcendentals=0,
    )
    vmem = pl.BlockSpec(memory_space=pltpu.VMEM)
    result = pl.pallas_call(
        kernel,
        out_shape=tuple(outs),
        in_specs=[pl.BlockSpec(memory_space=pl.ANY)] * len(arrays)
        + [vmem] * (len(queries) + len(metas)),
        out_specs=tuple([vmem] * len(outs)),
        scratch_shapes=[
            pltpu.VMEM((len(blocks), rows + META, width), jnp.bfloat16),
            pltpu.SemaphoreType.DMA((len(blocks),)),
        ]
        + [pltpu.VMEM((8, q[1]), jnp.float32) for q in queries],
        compiler_params=pltpu.CompilerParams(vmem_limit_bytes=VMEM_LIMIT),
        cost_estimate=cost,
        name=name,
    )(*arrays, *[q[0] for q in queries], *metas)
    if any(both):
        return result[0], list(result[1:])
    return None, list(result)


def solution(mesh):
    nz, nx, ny, nc = physical(mesh)
    places = [
        (z, x, y, c) for z in range(nz) for x in range(nx) for y in range(ny) for c in range(nc)
    ]

    def index(z, x, y, c):
        return (((z % nz) * nx + x % nx) * ny + y % ny) * nc + c % nc

    def shift(value, dx, dy, dc):
        perm = [(index(*p), index(p[0], p[1] - dx, p[2] - dy, p[3] - dc)) for p in places]
        return lax.ppermute(value, AXES, perm)

    def along(value, moves, back=False):
        perm = [
            (index(a, x, y, c), index(b, x, y, c))
            for a, b in moves
            for x in range(nx)
            for y in range(ny)
            for c in range(nc)
        ]
        return lax.ppermute(value, AXES, [(t, s) for s, t in perm] if back else perm)

    rounds = [[(a, (a + s) % nz) for a in range(nz)] for s in range(1, (nz + 1) // 2)]
    if nz % 2 == 0:
        s = nz // 2
        rounds.append([(a, a + s) if a % 2 == 0 else (a + s, a) for a in range(s)])
    offsets = [(dx, dy) for dx in range(nx) for dy in range(ny)]
    straight = [o for o in offsets[1:] if 0 in o]
    slanted = [o for o in offsets[1:] if 0 not in o]

    def local(embeddings, cluster_ids, rank_key):
        rows = embeddings.shape[0]
        half = rows // 2
        whole, low, high = prepare(embeddings, cluster_ids, rank_key)
        early = [along(whole, moves) for moves in rounds[:-1]]
        last_high = along(high, rounds[-1]) if rounds else None
        last_low = along(low, rounds[-1]) if rounds else None
        plane = {(0, 0, 0): [whole]}
        for dx, dy in straight:
            plane[dx, dy, 0] = [shift(whole, dx, dy, 0)]
        for dc in range(1, nc):
            plane[0, 0, dc] = [shift(whole, 0, 0, dc)]
        for dx, dy in slanted:
            plane[dx, dy, 0] = [
                shift(plane[dx, 0, 0][0][:half], 0, dy, 0),
                shift(plane[0, dy, 0][0][half:], dx, 0, 0),
            ]
        for dx, dy in straight + slanted:
            for dc in range(1, nc):
                plane[dx, dy, dc] = [shift(p, 0, 0, dc) for p in plane[dx, dy, 0]]

        own = (whole, rows, 0, None, False)
        found = {key: [] for key in plane}
        mine = []
        back = [[] for _ in rounds]

        def score(keys, queries, which, name):
            to_blocks, to_queries = pairs([plane[k] for k in keys], queries, name)
            if to_blocks is not None:
                for i, k in enumerate(keys):
                    found[k].append(to_blocks[i])
            for place, value in zip(which, to_queries):
                (mine if place is None else back[place]).append(value)

        here = [(0, 0, dc) for dc in range(nc)]
        near = [(dx, dy, dc) for dx, dy in straight for dc in range(nc)]
        far = [(dx, dy, dc) for dx, dy in slanted for dc in range(nc)]
        columns_ = [(block, rows, 0, None, True) for block in early]
        places_ = list(range(len(early)))
        score(here, [own], [None], "own")
        if early:
            score(here, columns_, places_, "column")
        if near:
            score(near, [own] + columns_, [None] + places_, "near")
        if far:
            score(far, [own] + columns_, [None] + places_, "far")
        tail = {}
        if rounds:
            everything = here + near + far
            for piece, n, first, meta, name in (
                (last_high, rows - half, half, None, "high"),
                (last_low, half, 0, last_high, "low"),
            ):
                to_blocks, to_queries = pairs(
                    [plane[k] for k in everything], [(piece, n, first, meta, True)], name
                )
                for i, k in enumerate(everything):
                    found[k].append(to_blocks[i])
                tail[name] = to_queries[0]

        top = functools.partial(functools.reduce, jnp.maximum)
        result = {k: top(v) for k, v in found.items() if v}
        for dc in range(1, nc):
            keys = [k for k in result if k[2] == dc]
            if keys:
                sent = shift(jnp.concatenate([result[k] for k in keys], axis=0), 0, 0, -dc)
                for i, (dx, dy, _) in enumerate(keys):
                    result[dx, dy, 0] = jnp.maximum(result[dx, dy, 0], sent[i : i + 1])
        for (dx, dy, dc), value in result.items():
            if dc == 0:
                mine.append(value if (dx, dy) == (0, 0) else shift(value, -dx, -dy, 0))
        z = lax.axis_index("grp") // nx
        for i, moves in enumerate(rounds):
            value = top(back[i]) if i < len(rounds) - 1 else jnp.concatenate([tail["low"], tail["high"]], axis=1)
            value = along(value, moves, back=True)
            if len(moves) < nz:
                sender = functools.reduce(jnp.logical_or, [z == a for a, _ in moves])
                value = jnp.where(sender, value, -1.0)
            mine.append(value)
        return top(mine).reshape(rows)

    placed = (P(AXES, None), P(AXES), P(AXES))
    return jax.shard_map(local, mesh=mesh, in_specs=placed, out_specs=P(AXES), check_vma=False)
```
